32 devices in a mesh: seq: 8 (over z, y), fsdp: 4 (over x, core).
Axes of the slice: x: 2, y: 2, z: 4, core: 2. Of those that a mesh axis runs over, the one named last changes fastest.
Arguments:
- block_in: float32 [4, 1024, 1024], P('fsdp', 'seq'), may hold values from -6 to 6
- cot: float32 [4, 1024, 1024], P('fsdp', 'seq'), may hold values from -6 to 6
- doc_ids: int32 [4, 1024], P('fsdp'), may hold values from 0 to 1, as said below
- positions: int32 [4, 1024], P('fsdp'), may hold values from 0 to 1022, as said below
- in_proj: float32 [1024, 8, 768], P('fsdp', 'seq'), may hold values from -0.1875 to 0.1875
- in_mean: float32 [1024, 8, 768], P('fsdp', 'seq'), may hold values from -15 to 15
- in_square: float32 [1024, 8, 768], P('fsdp', 'seq'), may hold values from 20 to 400
- gate_proj: float32 [1024, 8, 2], P('fsdp', 'seq'), may hold values from -0.1875 to 0.1875
- gate_mean: float32 [1024, 8, 2], P('fsdp', 'seq'), may hold values from -15 to 15
- gate_square: float32 [1024, 8, 2], P('fsdp', 'seq'), may hold values from 20 to 400
- conv_taps: float32 [4, 8, 512], P(None, 'seq', 'fsdp'), may hold values from -3 to 3
- conv_mean: float32 [4, 8, 512], P(None, 'seq', 'fsdp'), may hold values from -15 to 15
- conv_square: float32 [4, 8, 512], P(None, 'seq', 'fsdp'), may hold values from 20 to 400
- out_proj: float32 [8, 256, 1024], P('seq', None, 'fsdp'), may hold values from -0.125 to 0.125
- out_mean: float32 [8, 256, 1024], P('seq', None, 'fsdp'), may hold values from -15 to 15
- out_square: float32 [8, 256, 1024], P('seq', None, 'fsdp'), may hold values from 20 to 400
- ffn_up: float32 [1024, 2, 2816], P('fsdp', None, 'seq'), may hold values from -0.1875 to 0.1875
- up_mean: float32 [1024, 2, 2816], P('fsdp', None, 'seq'), may hold values from -15 to 15
- up_square: float32 [1024, 2, 2816], P('fsdp', None, 'seq'), may hold values from 20 to 400
- ffn_down: float32 [2816, 1024], P('seq', 'fsdp'), may hold values from -0.109375 to 0.109375
- down_mean: float32 [2816, 1024], P('seq', 'fsdp'), may hold values from -15 to 15
- down_square: float32 [2816, 1024], P('seq', 'fsdp'), may hold values from 20 to 400
- norm_gains: float32 [2, 1024], replicated, may hold values from 0.5 to 1.5
- gains_mean: float32 [2, 1024], replicated, may hold values from -15 to 15
- gains_square: float32 [2, 1024], replicated, may hold values from 20 to 400
- head_gain: float32 [256], replicated, may hold values from 0.5 to 1.5
- head_mean: float32 [256], replicated, may hold values from -15 to 15
- head_square: float32 [256], replicated, may hold values from 20 to 400
- decay_log: float32 [8], replicated, may hold values from 0 to 2.77
- decay_mean: float32 [8], replicated, may hold values from -15 to 15
- decay_square: float32 [8], replicated, may hold values from 20 to 400
- step_bias: float32 [8], replicated, may hold values from -7 to -3
- bias_mean: float32 [8], replicated, may hold values from -15 to 15
- bias_square: float32 [8], replicated, may hold values from 20 to 400
Outputs:
- block_out: float32 [4, 1024, 1024], P('fsdp', 'seq')
- grad_input: float32 [4, 1024, 1024], P('fsdp', 'seq')
- in_grad: float32 [1024, 8, 768], P('fsdp', 'seq')
- next_in_proj: float32 [1024, 8, 768], P('fsdp', 'seq')
- next_in_mean: float32 [1024, 8, 768], P('fsdp', 'seq')
- next_in_square: float32 [1024, 8, 768], P('fsdp', 'seq')
- gate_grad: float32 [1024, 8, 2], P('fsdp', 'seq')
- next_gate_proj: float32 [1024, 8, 2], P('fsdp', 'seq')
- next_gate_mean: float32 [1024, 8, 2], P('fsdp', 'seq')
- next_gate_square: float32 [1024, 8, 2], P('fsdp', 'seq')
- conv_grad: float32 [4, 8, 512], P(None, 'seq', 'fsdp')
- next_conv_taps: float32 [4, 8, 512], P(None, 'seq', 'fsdp')
- next_conv_mean: float32 [4, 8, 512], P(None, 'seq', 'fsdp')
- next_conv_square: float32 [4, 8, 512], P(None, 'seq', 'fsdp')
- out_grad: float32 [8, 256, 1024], P('seq', None, 'fsdp')
- next_out_proj: float32 [8, 256, 1024], P('seq', None, 'fsdp')
- next_out_mean: float32 [8, 256, 1024], P('seq', None, 'fsdp')
- next_out_square: float32 [8, 256, 1024], P('seq', None, 'fsdp')
- up_grad: float32 [1024, 2, 2816], P('fsdp', None, 'seq')
- next_ffn_up: float32 [1024, 2, 2816], P('fsdp', None, 'seq')
- next_up_mean: float32 [1024, 2, 2816], P('fsdp', None, 'seq')
- next_up_square: float32 [1024, 2, 2816], P('fsdp', None, 'seq')
- down_grad: float32 [2816, 1024], P('seq', 'fsdp')
- next_ffn_down: float32 [2816, 1024], P('seq', 'fsdp')
- next_down_mean: float32 [2816, 1024], P('seq', 'fsdp')
- next_down_square: float32 [2816, 1024], P('seq', 'fsdp')
- gains_grad: float32 [2, 1024], replicated
- next_norm_gains: float32 [2, 1024], replicated
- next_gains_mean: float32 [2, 1024], replicated
- next_gains_square: float32 [2, 1024], replicated
- head_grad: float32 [256], replicated
- next_head_gain: float32 [256], replicated
- next_head_mean: float32 [256], replicated
- next_head_square: float32 [256], replicated
- decay_grad: float32 [8], replicated
- next_decay_log: float32 [8], replicated
- next_decay_mean: float32 [8], replicated
- next_decay_square: float32 [8], replicated
- bias_grad: float32 [8], replicated
- next_step_bias: float32 [8], replicated
- next_bias_mean: float32 [8], replicated
- next_bias_square: float32 [8], replicated
The draws below stay inside these ranges and needn't reach their ends.
Inputs may be any that keep to these rules, and one draw needn't show every extreme that they name: `doc_ids`: each row holds two documents: id 0 up to a boundary between 1 and 1023 tokens in, id 1 after it. `positions`: positions count from 0 at the start of each document of the row, as doc_ids give them; some row has a document of 1023 tokens.
All inputs are finite; a program needn't handle non-finite values.
Results may differ from the reference program's by a relative error of at most 0.02.
The reference program's roundings to bfloat16 on the way count: a program that leaves them out, or rounds other values in their place, can miss the bound.
Values may be sent and summed in bfloat16 or wider, within the bound.
No kernel may reach another device: no remote copies, remote signals or barrier semaphores. Data moves between devices by JAX's collectives and lax.ppermute only.
A program may use at most 256 MiB of HBM per device.

```python
import math
import jax
import jax.numpy as jnp
from jax import lax

D = 1024
DK = 128
DV = 256
FF = 2816
KW = 4
SPAN = 64
STEP = 4
HEADS = 8
GROUP = 1024
BATCH = 4


def document_layout(key):
    boundary = jax.random.randint(jax.random.fold_in(key, 7), (BATCH, 1), 1, GROUP)
    chosen_row = jax.random.randint(jax.random.fold_in(key, 11), (), 0, BATCH)
    which_end = jax.random.randint(jax.random.fold_in(key, 13), (), 0, 2)
    extreme = jnp.where(which_end == 0, 1, GROUP - 1).astype(jnp.int32)
    row_ids = jnp.arange(BATCH, dtype=jnp.int32)[:, None]
    boundary = jnp.where(row_ids == chosen_row, extreme, boundary).astype(jnp.int32)
    places = jnp.arange(GROUP, dtype=jnp.int32)[None, :]
    documents = (places >= boundary).astype(jnp.int32)
    offsets = jnp.where(documents == 0, places, places - boundary).astype(jnp.int32)
    return (documents, offsets)


def draw_doc_ids(key, part):
    documents, offsets = document_layout(key)
    return documents


def draw_positions(key, part):
    documents, offsets = document_layout(key)
    return offsets


def steps_of(stream_key, dims, cuts, low, largest):
    def one(dim, blocks):
        draws = jax.random.uniform(jax.random.fold_in(jax.random.fold_in(stream_key, 6), dim), (blocks,), jnp.float32, low / len(cuts), largest / len(cuts))
        return jnp.repeat(jnp.exp(draws), dims[dim] // blocks).reshape((-1,) + (1,) * (len(dims) - dim - 1))

    factor_of = one(*cuts[0])
    for cut in cuts[1:]:
        factor_of = factor_of * one(*cut)
    return factor_of


def noise(own_key, extent, scale, reach, split=(), kind=jnp.bfloat16):
    drawn = scale * jax.random.normal(own_key, extent, jnp.float32)
    if split:
        drawn = drawn * steps_of(own_key, extent, split, -0.22, 0.18)
    return jnp.clip(drawn, -reach, reach).astype(kind)


def setup_inputs(seed: int = 0) -> dict:
    key_list = jax.random.split(jax.random.key(seed), 35)
    return {
        "block_in": noise(key_list[0], (BATCH, GROUP, D), 1.0, 6.0, ((0, 4), (1, 8)), jnp.float32),
        "cot": noise(key_list[1], (BATCH, GROUP, D), 1.0, 6.0, ((0, 4), (1, 8)), jnp.float32),
        "doc_ids": draw_doc_ids(jax.random.fold_in(key_list[34], 71), 0),
        "positions": draw_positions(jax.random.fold_in(key_list[34], 71), 0),
        "in_proj": noise(key_list[4], (D, HEADS, 2 * DK + 2 * DV), D ** -0.5, 0.1875, ((0, 4), (1, 8)), jnp.float32),
        "in_mean": noise(key_list[5], (D, HEADS, 2 * DK + 2 * DV), 3.0, 15.0, ((0, 4), (1, 8)), jnp.float32),
        "in_square": jnp.clip(jnp.exp(math.log(400.0) - 2.9957323 * jax.random.uniform(key_list[6], (D, HEADS, 2 * DK + 2 * DV), jnp.float32) ** steps_of(key_list[6], (D, HEADS, 2 * DK + 2 * DV), ((0, 4), (1, 8)), -0.2, 0.2)), 20.0, 400.0),
        "gate_proj": noise(key_list[7], (D, HEADS, 2), D ** -0.5, 0.1875, ((0, 4), (1, 8)), jnp.float32),
        "gate_mean": noise(key_list[8], (D, HEADS, 2), 3.0, 15.0, ((0, 4), (1, 8)), jnp.float32),
        "gate_square": jnp.clip(jnp.exp(math.log(400.0) - 2.9957323 * jax.random.uniform(key_list[9], (D, HEADS, 2), jnp.float32) ** steps_of(key_list[9], (D, HEADS, 2), ((0, 4), (1, 8)), -0.2, 0.2)), 20.0, 400.0),
        "conv_taps": noise(key_list[10], (KW, HEADS, 2 * DK + DV), 0.5, 3.0, ((1, 8), (2, 4)), jnp.float32),
        "conv_mean": noise(key_list[11], (KW, HEADS, 2 * DK + DV), 3.0, 15.0, ((1, 8), (2, 4)), jnp.float32),
        "conv_square": jnp.clip(jnp.exp(math.log(400.0) - 2.9957323 * jax.random.uniform(key_list[12], (KW, HEADS, 2 * DK + DV), jnp.float32) ** steps_of(key_list[12], (KW, HEADS, 2 * DK + DV), ((1, 8), (2, 4)), -0.2, 0.2)), 20.0, 400.0),
        "out_proj": noise(key_list[13], (HEADS, DV, D), (HEADS * DV) ** -0.5, 0.125, ((0, 8), (2, 4)), jnp.float32),
        "out_mean": noise(key_list[14], (HEADS, DV, D), 3.0, 15.0, ((0, 8), (2, 4)), jnp.float32),
        "out_square": jnp.clip(jnp.exp(math.log(400.0) - 2.9957323 * jax.random.uniform(key_list[15], (HEADS, DV, D), jnp.float32) ** steps_of(key_list[15], (HEADS, DV, D), ((0, 8), (2, 4)), -0.2, 0.2)), 20.0, 400.0),
        "ffn_up": noise(key_list[16], (D, 2, FF), D ** -0.5, 0.1875, ((0, 4), (2, 8)), jnp.float32),
        "up_mean": noise(key_list[17], (D, 2, FF), 3.0, 15.0, ((0, 4), (2, 8)), jnp.float32),
        "up_square": jnp.clip(jnp.exp(math.log(400.0) - 2.9957323 * jax.random.uniform(key_list[18], (D, 2, FF), jnp.float32) ** steps_of(key_list[18], (D, 2, FF), ((0, 4), (2, 8)), -0.2, 0.2)), 20.0, 400.0),
        "ffn_down": noise(key_list[19], (FF, D), FF ** -0.5, 0.109375, ((0, 8), (1, 4)), jnp.float32),
        "down_mean": noise(key_list[20], (FF, D), 3.0, 15.0, ((0, 8), (1, 4)), jnp.float32),
        "down_square": jnp.clip(jnp.exp(math.log(400.0) - 2.9957323 * jax.random.uniform(key_list[21], (FF, D), jnp.float32) ** steps_of(key_list[21], (FF, D), ((0, 8), (1, 4)), -0.2, 0.2)), 20.0, 400.0),
        "norm_gains": jnp.clip(1.0 + 0.1 * jax.random.normal(key_list[22], (2, D), jnp.float32), 0.5, 1.5),
        "gains_mean": noise(key_list[23], (2, D), 3.0, 15.0, (), jnp.float32),
        "gains_square": jnp.clip(jnp.exp(jax.random.uniform(key_list[24], (2, D), jnp.float32, math.log(20.0), math.log(400.0))), 20.0, 400.0),
        "head_gain": jnp.clip(1.0 + 0.1 * jax.random.normal(key_list[25], (DV,), jnp.float32), 0.5, 1.5),
        "head_mean": noise(key_list[26], (DV,), 3.0, 15.0, (), jnp.float32),
        "head_square": jnp.clip(jnp.exp(jax.random.uniform(key_list[27], (DV,), jnp.float32, math.log(20.0), math.log(400.0))), 20.0, 400.0),
        "decay_log": jnp.clip(jax.random.uniform(key_list[28], (HEADS,), jnp.float32, 0.0, 2.77), 0.0, 2.77),
        "decay_mean": noise(key_list[29], (HEADS,), 3.0, 15.0, (), jnp.float32),
        "decay_square": jnp.clip(jnp.exp(jax.random.uniform(key_list[30], (HEADS,), jnp.float32, math.log(20.0), math.log(400.0))), 20.0, 400.0),
        "step_bias": jnp.clip(jax.random.uniform(key_list[31], (HEADS,), jnp.float32, -7.0, -3.0), -7.0, -3.0),
        "bias_mean": noise(key_list[32], (HEADS,), 3.0, 15.0, (), jnp.float32),
        "bias_square": jnp.clip(jnp.exp(jax.random.uniform(key_list[33], (HEADS,), jnp.float32, math.log(20.0), math.log(400.0))), 20.0, 400.0),
    }


norm_eps = 1e-06
first_beta = 0.9
second_beta = 0.95
adam_eps = 1e-08
learn_rate = 0.01
weight_decay = 0.1
HIGHEST = lax.Precision.HIGHEST

def rms_scale(values, gain):
    return values * lax.rsqrt(lax.optimization_barrier(jnp.mean(values * values, axis=-1, keepdims=True)) + norm_eps) * gain

def swish(values):
    return values * jax.nn.sigmoid(values)

def through_bf16(values):
    return lax.optimization_barrier(values.astype(jnp.bfloat16)).astype(jnp.float32)

def head_mixer(projected, gate_pre, taps, decay_rate, step_shift, head_scale, token_pos, documents):
    length = projected.shape[0]
    conv_width = 2 * DK + DV
    conv_input = projected[:, :conv_width]
    output_gate = projected[:, conv_width:]
    filtered = conv_input * taps[0]
    for shift_by in range(1, KW):
        earlier = jnp.pad(conv_input[:length - shift_by], ((shift_by, 0), (0, 0)))
        usable = (token_pos >= shift_by).astype(jnp.float32)[:, None]
        filtered = filtered + earlier * taps[shift_by] * usable
    filtered = swish(filtered)
    queries = filtered[:, :DK]
    keys_unit = filtered[:, DK:2 * DK]
    values_in = filtered[:, 2 * DK:]
    queries = queries * lax.rsqrt(lax.optimization_barrier(jnp.sum(queries * queries, axis=-1, keepdims=True)) + norm_eps) * DK ** (-0.5)
    keys_unit = keys_unit * lax.rsqrt(lax.optimization_barrier(jnp.sum(keys_unit * keys_unit, axis=-1, keepdims=True)) + norm_eps)
    strength = jax.nn.sigmoid(gate_pre[:, 0])
    log_decay = -jnp.exp(decay_rate) * jax.nn.softplus(gate_pre[:, 1] + step_shift)
    blocks = length // SPAN
    queries = queries.reshape(blocks, SPAN, DK)
    keys_unit = keys_unit.reshape(blocks, SPAN, DK)
    values_in = values_in.reshape(blocks, SPAN, DV)
    strength = strength.reshape(blocks, SPAN)
    cumulative = jnp.cumsum(log_decay.reshape(blocks, SPAN), axis=1)
    block_docs = documents.reshape(blocks, SPAN)
    before_doc = jnp.concatenate([block_docs[:1, 0], block_docs[:-1, -1]])
    same_doc = block_docs[:, :, None] == block_docs[:, None, :]
    reaches = (block_docs == before_doc[:, None]).astype(jnp.float32)
    row_index = lax.broadcasted_iota(jnp.int32, (SPAN, SPAN), 0)
    col_index = lax.broadcasted_iota(jnp.int32, (SPAN, SPAN), 1)
    lower = row_index >= col_index
    strict = (row_index > col_index).astype(jnp.float32)
    gap_log = cumulative[:, :, None] - cumulative[:, None, :]
    decays = jnp.exp(jnp.where(lower, gap_log, 0.0)) * (same_doc & lower).astype(jnp.float32)
    weighted = decays * strength[:, None, :]
    key_inner = jnp.einsum('nid,njd->nij', keys_unit, keys_unit, precision=HIGHEST)
    system = jnp.eye(SPAN, dtype=jnp.float32) + key_inner * weighted * strict
    entry = jnp.exp(cumulative) * reaches
    solved = jax.scipy.linalg.solve_triangular(system, jnp.concatenate([keys_unit * entry[..., None], values_in], axis=-1), lower=True, unit_diagonal=True)
    carry_w = solved[..., :DK]
    carry_u = solved[..., DK:]
    scores = jnp.einsum('nid,njd->nij', queries, keys_unit, precision=HIGHEST) * weighted
    keys_last = keys_unit * weighted[:, -1, :][..., None]
    entry_last = entry[:, -1]

    def advance(state, item):
        block_w, block_u, block_q, block_e, block_s, block_k, block_l = item
        fresh = block_u - jnp.dot(block_w, state, precision=HIGHEST)
        output = block_e[:, None] * jnp.dot(block_q, state, precision=HIGHEST) + jnp.dot(block_s, fresh, precision=HIGHEST)
        state = block_l * state + jnp.dot(block_k.T, fresh, precision=HIGHEST)
        return (state, output)
    start_state = jnp.zeros((DK, DV), jnp.float32)
    _, reads = lax.scan(advance, start_state, (carry_w, carry_u, queries, entry, scores, keys_last, entry_last))
    reads = reads.reshape(length, DV)
    return rms_scale(reads, head_scale) * swish(output_gate)

def all_heads(projected, gate_pre, taps, decay_rate, step_shift, head_scale, token_pos, documents):
    mapped = jax.vmap(head_mixer, in_axes=(1, 1, 1, 0, 0, None, None, None), out_axes=1)
    return mapped(projected, gate_pre, taps, decay_rate, step_shift, head_scale, token_pos, documents)

def adam_step(weight, mean, square, grad):
    mean_next = first_beta * mean + (1.0 - first_beta) * grad
    square_next = second_beta * square + (1.0 - second_beta) * grad * grad
    mean_hat = mean_next / (1.0 - first_beta ** STEP)
    square_hat = square_next / (1.0 - second_beta ** STEP)
    weight_next = weight - learn_rate * (mean_hat / (jnp.sqrt(square_hat) + adam_eps) + weight_decay * weight)
    return (weight_next, mean_next, square_next)

def reference(block_in, cot, doc_ids, positions, in_proj, in_mean, in_square, gate_proj, gate_mean, gate_square, conv_taps, conv_mean, conv_square, out_proj, out_mean, out_square, ffn_up, up_mean, up_square, ffn_down, down_mean, down_square, norm_gains, gains_mean, gains_square, head_gain, head_mean, head_square, decay_log, decay_mean, decay_square, step_bias, bias_mean, bias_square):
    in_weight = through_bf16(in_proj)
    gate_weight = through_bf16(gate_proj)
    taps_weight = through_bf16(conv_taps)
    out_weight = through_bf16(out_proj)
    up_weight = through_bf16(ffn_up)
    down_weight = through_bf16(ffn_down)

    def one_row(totals, item):
        row_in, row_cot, row_doc, row_pos = item
        normed, norm_pull = jax.vjp(rms_scale, row_in, norm_gains[0])
        normed_half = through_bf16(normed)
        projected = jnp.einsum('td,dhc->thc', normed_half, in_weight, precision=HIGHEST)
        gate_pre = jnp.einsum('td,dhc->thc', normed_half, gate_weight, precision=HIGHEST)

        def heads_fn(proj_in, gate_in, taps_in, rate_in, shift_in, scale_in):
            return all_heads(proj_in, gate_in, taps_in, rate_in, shift_in, scale_in, row_pos, row_doc)
        mixed, mixer_pull = jax.vjp(heads_fn, projected, gate_pre, taps_weight, decay_log, step_bias, head_gain)
        mixed_half = through_bf16(mixed)
        hidden = row_in + jnp.einsum('thv,hvd->td', mixed_half, out_weight, precision=HIGHEST)
        normed2, norm2_pull = jax.vjp(rms_scale, hidden, norm_gains[1])
        normed2_half = through_bf16(normed2)
        pre = jnp.einsum('td,dgf->tgf', normed2_half, up_weight, precision=HIGHEST)
        pre_gate = pre[:, 0]
        pre_up = pre[:, 1]
        sigma = jax.nn.sigmoid(pre_gate)
        act_half = through_bf16(pre_gate * sigma * pre_up)
        block_row = hidden + jnp.einsum('tf,fd->td', act_half, down_weight, precision=HIGHEST)
        cot_half = through_bf16(row_cot)
        d_act = jnp.einsum('td,fd->tf', cot_half, down_weight, precision=HIGHEST)
        down_part = jnp.einsum('tf,td->fd', act_half, cot_half, precision=HIGHEST)
        d_gate = d_act * pre_up * sigma * (1.0 + pre_gate * (1.0 - sigma))
        d_up = d_act * pre_gate * sigma
        d_pre = through_bf16(jnp.stack([d_gate, d_up], axis=1))
        up_part = jnp.einsum('td,tgf->dgf', normed2_half, d_pre, precision=HIGHEST)
        d_normed2 = jnp.einsum('tgf,dgf->td', d_pre, up_weight, precision=HIGHEST)
        hidden_part, gain_two = norm2_pull(d_normed2)
        d_hidden = row_cot + hidden_part
        d_hidden_half = through_bf16(d_hidden)
        out_part = jnp.einsum('thv,td->hvd', mixed_half, d_hidden_half, precision=HIGHEST)
        d_mixed = jnp.einsum('td,hvd->thv', d_hidden_half, out_weight, precision=HIGHEST)
        d_proj, d_gates, taps_part, decay_part, bias_part, head_part = mixer_pull(d_mixed)
        d_proj_half = through_bf16(d_proj)
        d_gates_half = through_bf16(d_gates)
        in_part = jnp.einsum('td,thc->dhc', normed_half, d_proj_half, precision=HIGHEST)
        gate_part = jnp.einsum('td,thc->dhc', normed_half, d_gates_half, precision=HIGHEST)
        d_normed = jnp.einsum('thc,dhc->td', d_proj_half, in_weight, precision=HIGHEST) + jnp.einsum('thc,dhc->td', d_gates_half, gate_weight, precision=HIGHEST)
        input_part, gain_one = norm_pull(d_normed)
        input_row = d_hidden + input_part
        parts = (in_part, gate_part, taps_part, out_part, up_part, down_part, jnp.stack([gain_one, gain_two]), head_part, decay_part, bias_part)
        totals = tuple((total + part for total, part in zip(totals, parts)))
        return (totals, (block_row, input_row))
    params = (in_proj, gate_proj, conv_taps, out_proj, ffn_up, ffn_down, norm_gains, head_gain, decay_log, step_bias)
    means = (in_mean, gate_mean, conv_mean, out_mean, up_mean, down_mean, gains_mean, head_mean, decay_mean, bias_mean)
    squares = (in_square, gate_square, conv_square, out_square, up_square, down_square, gains_square, head_square, decay_square, bias_square)
    start = tuple((jnp.zeros(param.shape, jnp.float32) for param in params))
    grads, (block_rows, input_rows) = lax.scan(one_row, start, (block_in, cot, doc_ids, positions))
    results = [block_rows, input_rows]
    for param, mean, square, grad in zip(params, means, squares, grads):
        weight_next, mean_next, square_next = adam_step(param, mean, square, grad)
        results.extend([grad, weight_next, mean_next, square_next])
    return tuple(results)
```

```python
import jax
import jax.numpy as jnp
from jax import lax
from jax.sharding import PartitionSpec as P
from jax.experimental import pallas as pl
from jax.experimental.pallas import tpu as pltpu

KW = 4
norm_eps = 1e-06
CHUNK = 128
LEAF = 16
f32 = jnp.float32
bf16 = jnp.bfloat16


def split(a):
    hi = a.astype(bf16)
    return hi, (a - hi.astype(f32)).astype(bf16)


def dot3(a, b, ca=1, cb=0):
    dims = (((ca,), (cb,)), ((), ()))
    ah, al = a if isinstance(a, tuple) else split(a)
    bh, bl = b if isinstance(b, tuple) else split(b)
    dg = lambda x, y: lax.dot_general(x, y, dims, preferred_element_type=f32)
    return dg(ah, bh) + (dg(ah, bl) + dg(al, bh))


def iotas():
    row = lax.broadcasted_iota(jnp.int32, (CHUNK, CHUNK), 0)
    col = lax.broadcasted_iota(jnp.int32, (CHUNK, CHUNK), 1)
    return row, col


def to_col(row_vec, eye):
    return jnp.sum(jnp.where(eye, row_vec, 0.0), axis=1, keepdims=True)


def to_row(col_vec, eye):
    return jnp.sum(jnp.where(eye, col_vec, 0.0), axis=0, keepdims=True)


def unit_inverse(a, row, col):
    size = LEAF
    same = (row // size) == (col // size)
    leaf = jnp.where(same, a, 0.0)
    inv = jnp.where(row == col, 1.0, 0.0) - leaf
    power = leaf
    done = 2
    while done < size:
        power_s = split(power)
        power = dot3(power_s, power_s)
        inv = inv + dot3(inv, power)
        done *= 2
    while size < CHUNK:
        wider = (row // (2 * size)) == (col // (2 * size))
        off = jnp.where(wider & jnp.logical_not(same), a, 0.0)
        inv_s = split(inv)
        inv = inv - dot3(inv_s, dot3(off, inv_s))
        same = wider
        size *= 2
    return inv


def gate_values(rows_ref, c, n, scal_ref):
    sl = pl.ds(pl.multiple_of(c * CHUNK, CHUNK), CHUNK)
    row, col = iotas()
    eye = row == col
    lower = row >= col
    blk = rows_ref[:, sl]
    logit, pre, doc, pos = blk[0:1], blk[1:2], blk[2:3], blk[3:4]
    before = jnp.maximum(c - 1, 0)
    prev = rows_ref[:, pl.ds(pl.multiple_of(before * CHUNK, CHUNK), CHUNK)][2:3]
    lane = lax.broadcasted_iota(jnp.int32, (1, CHUNK), 1)
    last = lane == CHUNK - 1
    before_doc = jnp.where(
        c > 0,
        jnp.sum(jnp.where(last, prev, 0.0), axis=1, keepdims=True),
        jnp.sum(jnp.where(lane == 0, doc, 0.0), axis=1, keepdims=True),
    )
    beta = jax.nn.sigmoid(logit)
    shifted = pre + scal_ref[1]
    soft = jnp.maximum(shifted, 0.0) + jnp.log1p(jnp.exp(-jnp.abs(shifted)))
    ld = scal_ref[0] * soft
    ld_col = to_col(ld, eye)
    g_col = jnp.sum(jnp.where(lower, ld, 0.0), axis=1, keepdims=True)
    g_row = jnp.sum(jnp.where(row <= col, ld_col, 0.0), axis=0, keepdims=True)
    doc_col = to_col(doc, eye)
    beta_col = to_col(beta, eye)
    live = lower & (doc_col == doc)
    decay = jnp.where(live, jnp.exp(jnp.where(lower, g_col - g_row, 0.0)), 0.0)
    weighted = decay * beta
    e_col = jnp.where(doc_col == before_doc, jnp.exp(g_col), 0.0)
    g_last = jnp.sum(jnp.where(last, g_row, 0.0), axis=1, keepdims=True)
    doc_last = jnp.sum(jnp.where(last, doc, 0.0), axis=1, keepdims=True)
    decay_last = jnp.where(doc_col == doc_last, jnp.exp(g_last - g_col), 0.0)
    e_last = jnp.where(doc_last == before_doc, jnp.exp(g_last), 0.0)
    return dict(
        row=row, col=col, eye=eye, lower=lower, beta=beta, beta_col=beta_col, shifted=shifted,
        ld=ld, decay=decay, weighted=weighted, e_col=e_col, decay_last=decay_last,
        e_last=e_last, pos_col=to_col(pos, eye),
    )


def conv_chunk(proj_ref, taps_ref, c, pos_col, width):
    start = pl.multiple_of(c * CHUNK, CHUNK)
    before = pl.multiple_of(jnp.maximum(c * CHUNK - 8, 0), 8)
    cur = proj_ref[pl.ds(start, CHUNK), :width]
    cat = jnp.concatenate([proj_ref[pl.ds(before, 8), :width], cur], axis=0)
    shifts = [cur]
    out = cur * taps_ref[0:1]
    for j in range(1, KW):
        earlier = jnp.where(pos_col >= j, pltpu.roll(cat, j, 0)[8:], 0.0)
        shifts.append(earlier)
        out = out + earlier * taps_ref[j : j + 1]
    return out, shifts


def forward_kernel(dk, dv, n, scal_ref, proj_ref, rows_ref, taps_ref, gain_ref,
                   mixed_ref, read_ref, qk_ref, t_ref, w_ref, f_ref, s_ref, m_ref, g_ref, h_ref,
                   u_scr, p_scr, n_scr):
    width = 2 * dk + dv
    scale = dk ** -0.5

    def first(c):
        sl = pl.ds(pl.multiple_of(c * CHUNK, CHUNK), CHUNK)
        gv = gate_values(rows_ref, c, n, scal_ref)
        pre, _ = conv_chunk(proj_ref, taps_ref, c, gv["pos_col"], width)
        filt = pre * jax.nn.sigmoid(pre)
        q, k, v = filt[:, :dk], filt[:, dk : 2 * dk], filt[:, 2 * dk :]
        q = q * lax.rsqrt(jnp.sum(q * q, axis=1, keepdims=True) + norm_eps) * scale
        k = k * lax.rsqrt(jnp.sum(k * k, axis=1, keepdims=True) + norm_eps)
        qk_ref[sl, :dk] = q
        qk_ref[sl, dk:] = k
        k_s = split(k)
        h = dot3(k_s, k_s, 1, 1)
        g = dot3(q, k_s, 1, 1)
        h_ref[c] = h
        g_ref[c] = g
        a = jnp.where(gv["row"] > gv["col"], h * gv["weighted"], 0.0)
        t = unit_inverse(a, gv["row"], gv["col"])
        t_ref[c] = t
        t_s = split(t)
        w = dot3(t_s, k * gv["e_col"])
        u = dot3(t_s, v)
        w_ref[sl, :] = w
        u_scr[sl, :] = u
        p_scr[c] = g * gv["weighted"]
        kl = split(k * (gv["decay_last"] * gv["beta_col"]))
        m_ref[c] = jnp.where(gv["eye"], gv["e_last"], 0.0) - dot3(kl, w, 0, 0)
        n_scr[c] = dot3(kl, u, 0, 0)

    def scan(c, state):
        s_ref[c] = state
        return dot3(m_ref[c], state) + n_scr[c]

    def last(c):
        sl = pl.ds(pl.multiple_of(c * CHUNK, CHUNK), CHUNK)
        gv = gate_values(rows_ref, c, n, scal_ref)
        state = split(s_ref[c])
        f = u_scr[sl, :] - dot3(w_ref[sl, :], state)
        f_ref[sl, :] = f
        read = dot3(qk_ref[sl, :dk] * gv["e_col"], state) + dot3(p_scr[c], f)
        read_ref[sl, :] = read
        og = proj_ref[sl, width:]
        normed = read * lax.rsqrt(jnp.mean(read * read, axis=1, keepdims=True) + norm_eps)
        mixed_ref[sl, :] = (normed * gain_ref[...] * (og * jax.nn.sigmoid(og))).astype(bf16)

    looped(n, first)
    lax.fori_loop(0, n, scan, jnp.zeros((dk, dv), f32))
    looped(n, last)


GROUP_OF = 2


def looped(n, body):
    step = GROUP_OF if n % GROUP_OF == 0 else 1

    def go(i, _):
        for j in range(step):
            body(i * step + j)
        return 0

    lax.fori_loop(0, n // step, go, 0)


def backward_kernel(dk, dv, n, scal_ref, proj_ref, rows_ref, taps_ref, gain_ref, dm_ref,
                    read_ref, qk_ref, t_ref, w_ref, f_ref, s_ref, m_ref, g_ref, h_ref,
                    dproj_ref, drows_ref, dtaps_ref, dsmall_ref,
                    do_scr, x_scr, n_scr, ds_scr, dpre_scr):
    width = 2 * dk + dv
    scale = dk ** -0.5

    def first(c, dgain):
        sl = pl.ds(pl.multiple_of(c * CHUNK, CHUNK), CHUNK)
        gv = gate_values(rows_ref, c, n, scal_ref)
        og = proj_ref[sl, width:]
        read = read_ref[sl, :]
        dm = dm_ref[sl, :]
        r = lax.rsqrt(jnp.mean(read * read, axis=1, keepdims=True) + norm_eps)
        y = read * r
        sig = jax.nn.sigmoid(og)
        gain = gain_ref[...]
        dz = dm * (og * sig)
        dproj_ref[sl, width:] = (dm * (y * gain) * (sig * (1.0 + og * (1.0 - sig)))).astype(bf16)
        dgain = dgain + jnp.sum(dz * y, axis=0, keepdims=True)
        dy = dz * gain
        d_o = r * (dy - y * jnp.mean(dy * y, axis=1, keepdims=True))
        do_scr[sl, :] = d_o
        do_s = split(d_o)
        x = dot3(g_ref[c] * gv["weighted"], do_s, 0, 0)
        x_scr[sl, :] = x
        n_scr[c] = dot3(qk_ref[sl, :dk] * gv["e_col"], do_s, 0, 0) - dot3(w_ref[sl, :], x, 0, 0)
        return dgain

    def scan(i, d_state):
        c = n - 1 - i
        ds_scr[c] = d_state
        return dot3(m_ref[c], d_state, 0, 0) + n_scr[c]

    def last(c, carry):
        dtaps, d_rate, d_shift = carry
        sl = pl.ds(pl.multiple_of(c * CHUNK, CHUNK), CHUNK)
        gv = gate_values(rows_ref, c, n, scal_ref)
        eye, lower = gv["eye"], gv["lower"]
        pre, shifts = conv_chunk(proj_ref, taps_ref, c, gv["pos_col"], width)
        sig = jax.nn.sigmoid(pre)
        filt = pre * sig
        qf, kf = filt[:, :dk], filt[:, dk : 2 * dk]
        rq = lax.rsqrt(jnp.sum(qf * qf, axis=1, keepdims=True) + norm_eps)
        rk = lax.rsqrt(jnp.sum(kf * kf, axis=1, keepdims=True) + norm_eps)
        q_hat = qf * rq
        k = kf * rk
        q = q_hat * scale
        beta_col, e_col, decay_last = gv["beta_col"], gv["e_col"], gv["decay_last"]
        w_last = decay_last * beta_col
        state, d_state = s_ref[c], ds_scr[c]
        state_s, d_state_s = split(state), split(d_state)
        d_f = x_scr[sl, :] + dot3(k * w_last, d_state_s)
        d_r = dot3(t_ref[c], d_f, 0, 0)
        dr_s, f_s, do_s = split(d_r), split(f_ref[sl, :]), split(do_scr[sl, :])
        d_a = jnp.where(gv["row"] > gv["col"], -dot3(dr_s, f_s, 1, 1), 0.0)
        d_p = dot3(do_s, f_s, 1, 1)
        d_ke = -dot3(dr_s, state_s, 1, 1)
        d_qe = dot3(do_s, state_s, 1, 1)
        d_kl = dot3(f_s, d_state_s, 1, 1)
        weighted = gv["weighted"]
        d_w = d_p * g_ref[c] + d_a * h_ref[c]
        d_g = split(d_p * weighted)
        d_h = d_a * weighted
        d_hh = d_h + d_h.T
        k_s = split(k)
        dq = dot3(d_g, k_s) + e_col * d_qe
        dk_ = dot3(d_g, q, 0, 0) + dot3(d_hh, k_s) + e_col * d_ke + w_last * d_kl
        d_wl = jnp.sum(d_kl * k, axis=1, keepdims=True)
        d_beta = jnp.sum(d_w * gv["decay"], axis=0, keepdims=True) + to_row(d_wl * decay_last, eye)
        d_gap = d_w * weighted
        t_last = d_wl * w_last
        d_e = jnp.sum(d_qe * q + d_ke * k, axis=1, keepdims=True)
        down = jnp.sum(d_gap, axis=0, keepdims=True)
        dg_col = jnp.sum(d_gap, axis=1, keepdims=True) - to_col(down, eye) - t_last + d_e * e_col
        tail = jnp.sum(t_last, axis=0, keepdims=True) + gv["e_last"] * jnp.sum(
            jnp.sum(d_state * state, axis=1, keepdims=True), axis=0, keepdims=True
        )
        d_ld = jnp.sum(jnp.where(lower, dg_col, 0.0), axis=0, keepdims=True) + tail
        beta = gv["beta"]
        d_logit = d_beta * beta * (1.0 - beta)
        d_pre_gate = d_ld * scal_ref[0] * jax.nn.sigmoid(gv["shifted"])
        drows_ref[0:1, sl] = d_logit
        drows_ref[1:2, sl] = d_pre_gate
        d_rate = d_rate + d_ld * gv["ld"]
        d_shift = d_shift + d_pre_gate
        dqs = dq * scale
        dqf = rq * (dqs - q_hat * jnp.sum(dqs * q_hat, axis=1, keepdims=True))
        dkf = rk * (dk_ - k * jnp.sum(dk_ * k, axis=1, keepdims=True))
        d_filt = jnp.concatenate([dqf, dkf, d_r], axis=1)
        d_pre = d_filt * (sig * (1.0 + pre * (1.0 - sig)))
        dpre_scr[sl, :] = d_pre
        dtaps = tuple(
            dtaps[j] + jnp.sum(d_pre * shifts[j], axis=0, keepdims=True) for j in range(KW)
        )
        return dtaps, d_rate, d_shift

    def conv_back(c):
        sl = pl.ds(pl.multiple_of(c * CHUNK, CHUNK), CHUNK)
        row, col = iotas()
        eye = row == col
        ext = pl.ds(pl.multiple_of(c * CHUNK, CHUNK), CHUNK + 8)
        cat = dpre_scr[ext, :]
        pos_col = to_col(rows_ref[:, sl][3:4], eye)
        nxt = pl.multiple_of(jnp.minimum(c + 1, n - 1) * CHUNK, CHUNK)
        pos_next = to_col(rows_ref[:, pl.ds(nxt, CHUNK)][3:4], eye)[:8]
        pos_cat = jnp.concatenate([pos_col, pos_next], axis=0)
        out = cat[:CHUNK] * taps_ref[0:1]
        for j in range(1, KW):
            ahead = jnp.where(pos_cat >= j, cat, 0.0)
            out = out + pltpu.roll(ahead, CHUNK + 8 - j, 0)[:CHUNK] * taps_ref[j : j + 1]
        dproj_ref[sl, :width] = out.astype(bf16)

    dpre_scr[pl.ds(n * CHUNK, 8), :] = jnp.zeros((8, width), f32)
    dgain = lax.fori_loop(0, n, first, jnp.zeros((1, dv), f32))
    lax.fori_loop(0, n, scan, jnp.zeros((dk, dv), f32))
    zero = jnp.zeros((1, CHUNK), f32)
    dtaps, d_rate, d_shift = lax.fori_loop(
        0, n, last, (tuple(jnp.zeros((1, width), f32) for _ in range(KW)), zero, zero)
    )
    looped(n, conv_back)
    for j in range(KW):
        dtaps_ref[j : j + 1] = dtaps[j]
    dsmall_ref[0:1] = dgain
    dsmall_ref[1:2] = jnp.broadcast_to(jnp.sum(d_rate, axis=1, keepdims=True), (1, dv))
    dsmall_ref[2:3] = jnp.broadcast_to(jnp.sum(d_shift, axis=1, keepdims=True), (1, dv))


VMEM_LIMIT = 60 * 1024 * 1024


def specs(n):
    return [pl.BlockSpec(memory_space=pltpu.SMEM)] + [
        pl.BlockSpec(memory_space=pltpu.VMEM) for _ in range(n)
    ]


def mixer_forward(dk, dv, scal, proj, rows, taps, gain):
    length = proj.shape[0]
    n = length // CHUNK
    sd = jax.ShapeDtypeStruct
    return pl.pallas_call(
        lambda *refs: forward_kernel(dk, dv, n, *refs),
        out_shape=(
            sd((length, dv), bf16), sd((length, dv), f32), sd((length, 2 * dk), f32),
            sd((n, CHUNK, CHUNK), f32), sd((length, dk), f32), sd((length, dv), f32),
            sd((n, dk, dv), f32), sd((n, dk, dk), f32), sd((n, CHUNK, CHUNK), f32),
            sd((n, CHUNK, CHUNK), f32),
        ),
        in_specs=specs(4),
        out_specs=specs(10)[1:],
        scratch_shapes=[
            pltpu.VMEM((length, dv), f32), pltpu.VMEM((n, CHUNK, CHUNK), f32),
            pltpu.VMEM((n, dk, dv), f32),
        ],
        compiler_params=pltpu.CompilerParams(vmem_limit_bytes=VMEM_LIMIT),
        name="mixer_forward",
    )(scal, proj, rows, taps, gain)


def mixer_backward(dk, dv, scal, proj, rows, taps, gain, dm, saved):
    length = proj.shape[0]
    n = length // CHUNK
    width = 2 * dk + dv
    sd = jax.ShapeDtypeStruct
    return pl.pallas_call(
        lambda *refs: backward_kernel(dk, dv, n, *refs),
        out_shape=(
            sd((length, width + dv), bf16), sd((2, length), f32), sd((KW, width), f32),
            sd((3, dv), f32),
        ),
        in_specs=specs(5 + len(saved)),
        out_specs=specs(4)[1:],
        scratch_shapes=[
            pltpu.VMEM((length, dv), f32), pltpu.VMEM((length, dv), f32),
            pltpu.VMEM((n, dk, dv), f32), pltpu.VMEM((n, dk, dv), f32),
            pltpu.VMEM((length + 8, width), f32),
        ],
        compiler_params=pltpu.CompilerParams(vmem_limit_bytes=VMEM_LIMIT),
        name="mixer_backward",
    )(scal, proj, rows, taps, gain, dm, *saved)


STEP = 4
first_beta = 0.9
second_beta = 0.95
adam_eps = 1e-08
learn_rate = 0.01
weight_decay = 0.1


def rms_scale(values, gain):
    return values * lax.rsqrt(jnp.mean(values * values, axis=-1, keepdims=True) + norm_eps) * gain


def dot(a, b, ca, cb):
    return lax.dot_general(a, b, (((ca,), (cb,)), ((), ())), preferred_element_type=f32)


def exchange(x, axis, mask):
    size = lax.axis_size(axis)
    return lax.ppermute(x, axis, [(j, j ^ mask) for j in range(size)])


def gather_pieces(x, axis):
    size = lax.axis_size(axis)
    pieces = [None] * size
    for k in range(0, size, 2):
        pieces[k] = x if k == 0 else exchange(x, axis, k)
    for k in range(0, size, 2):
        pieces[k + 1] = exchange(pieces[k], axis, 1)
    return pieces


def in_order(pieces, axis, dim):
    me = lax.axis_index(axis)
    part = pieces[0].shape[dim]
    shape = list(pieces[0].shape)
    shape[dim] = part * len(pieces)
    out = jnp.zeros(shape, pieces[0].dtype)
    for k, piece in enumerate(pieces):
        out = lax.dynamic_update_slice_in_dim(out, piece, (me ^ k) * part, dim)
    return out


def scatter_sum(block_for, axis):
    size = lax.axis_size(axis)
    total = None
    for k in list(range(2, size, 2)) + [0]:
        pair = block_for(k) + exchange(block_for(k + 1).astype(bf16), axis, 1).astype(f32)
        if k:
            pair = exchange(pair.astype(bf16), axis, k).astype(f32)
        total = pair if total is None else total + pair
    return total


def block_of(x, axis, dim):
    me = lax.axis_index(axis)
    part = x.shape[dim] // lax.axis_size(axis)
    return lambda k: lax.dynamic_slice_in_dim(x, (me ^ k) * part, part, dim).astype(f32)


def tree_sum(x, axis):
    size = lax.axis_size(axis)
    parts = [x] + [exchange(x, axis, k) for k in range(1, size)]
    while len(parts) > 1:
        parts = [parts[j] + parts[j + 1] for j in range(0, len(parts), 2)]
    return parts[0]


def adam_step(weight, mean, square, grad):
    mean_next = first_beta * mean + (1.0 - first_beta) * grad
    square_next = second_beta * square + (1.0 - second_beta) * grad * grad
    mean_hat = mean_next / (1.0 - first_beta**STEP)
    square_hat = square_next / (1.0 - second_beta**STEP)
    weight_next = weight - learn_rate * (
        mean_hat / (jnp.sqrt(square_hat) + adam_eps) + weight_decay * weight
    )
    return (weight_next, mean_next, square_next)


def per_device(
    block_in, cot, doc_ids, positions,
    in_proj, in_mean, in_square,
    gate_proj, gate_mean, gate_square,
    conv_taps, conv_mean, conv_square,
    out_proj, out_mean, out_square,
    ffn_up, up_mean, up_square,
    ffn_down, down_mean, down_square,
    norm_gains, gains_mean, gains_square,
    head_gain, head_mean, head_square,
    decay_log, decay_mean, decay_square,
    step_bias, bias_mean, bias_square,
):
    fsdp = lax.axis_size("fsdp")
    heads = in_proj.shape[1]
    columns = in_proj.shape[2]
    dv = head_gain.shape[0]
    dk = (columns - 2 * dv) // 2
    width = 2 * dk + dv
    rows_d = in_proj.shape[0]
    model = rows_d * fsdp
    units = ffn_up.shape[2]
    taps_d = conv_taps.shape[2]
    length = doc_ids.shape[1]
    head_start = lax.axis_index("seq") * heads

    own_rows = block_in[0]
    own_cot = cot[0]
    normed, norm_pull = jax.vjp(rms_scale, own_rows, norm_gains[0])
    rows_all = in_order(gather_pieces(normed.astype(bf16), "seq"), "seq", 0)

    small = jnp.concatenate(
        [
            gate_proj.transpose(1, 2, 0).reshape(1, -1),
            conv_taps.transpose(1, 0, 2).reshape(1, -1),
        ],
        axis=1,
    ).astype(bf16)
    in_full = in_order(
        gather_pieces(in_proj.reshape(rows_d, heads * columns).astype(bf16), "fsdp"), "fsdp", 0
    )
    small_all = in_order(gather_pieces(small, "fsdp"), "fsdp", 0)
    gate_size = heads * 2 * rows_d
    gate_full = (
        small_all[:, :gate_size]
        .reshape(fsdp, heads * 2, rows_d)
        .transpose(1, 0, 2)
        .reshape(heads * 2, model)
    )
    taps_full = (
        small_all[:, gate_size:]
        .reshape(fsdp, heads, KW, taps_d)
        .transpose(1, 2, 0, 3)
        .reshape(heads, KW, width)
        .astype(f32)
    )
    out_full = in_order(
        gather_pieces(out_proj.reshape(heads * dv, rows_d).astype(bf16), "fsdp"), "fsdp", 1
    )
    up_full = in_order(
        gather_pieces(ffn_up.transpose(1, 0, 2).astype(bf16), "fsdp"), "fsdp", 1
    )
    down_full = in_order(gather_pieces(ffn_down.astype(bf16), "fsdp"), "fsdp", 1)

    projected = dot(rows_all, in_full, 1, 0)
    gate_pre = dot(gate_full, rows_all, 1, 1)
    extra = jnp.concatenate([doc_ids, positions], axis=0).astype(f32)
    scal_all = jnp.stack([-jnp.exp(decay_log), step_bias])
    scal_here = lax.dynamic_slice_in_dim(scal_all, head_start, heads, 1)
    gain_row = head_gain[None]
    fronts = []
    for h in range(heads):
        proj_h = projected[:, h * columns : (h + 1) * columns]
        rows_h = jnp.concatenate([gate_pre[2 * h : 2 * h + 2], extra], axis=0)
        args = (scal_here[:, h], proj_h, rows_h, taps_full[h], gain_row)
        fronts.append((args, mixer_forward(dk, dv, *args)))
    mixed_half = jnp.concatenate([front[1][0] for front in fronts], axis=1)

    attn_part = dot(mixed_half, out_full, 1, 0).astype(bf16)
    hidden = own_rows + scatter_sum(block_of(attn_part, "seq", 0), "seq")
    normed2, norm2_pull = jax.vjp(rms_scale, hidden, norm_gains[1])

    cot_all = jnp.concatenate(gather_pieces(own_cot.astype(bf16), "seq"), axis=0)
    ffn_rows = jnp.concatenate(gather_pieces(normed2.astype(bf16), "seq"), axis=0)
    own = own_rows.shape[0]
    piece_of = lambda x: lambda k: x[k * own : (k + 1) * own].astype(f32)
    pre_gate = dot(ffn_rows, up_full[0], 1, 0)
    pre_up = dot(ffn_rows, up_full[1], 1, 0)
    sigma = jax.nn.sigmoid(pre_gate)
    act_half = (pre_gate * sigma * pre_up).astype(bf16)
    d_act = dot(cot_all, down_full, 1, 1)
    d_gate = (d_act * pre_up * sigma * (1.0 + pre_gate * (1.0 - sigma))).astype(bf16)
    d_up = (d_act * pre_gate * sigma).astype(bf16)
    d_normed2_part = (dot(d_gate, up_full[0], 1, 1) + dot(d_up, up_full[1], 1, 1)).astype(bf16)
    d_normed2 = scatter_sum(piece_of(d_normed2_part), "seq")
    hidden_part, gain_two = norm2_pull(d_normed2)
    d_hidden = own_cot + hidden_part
    dmix_all = in_order(gather_pieces(d_hidden.astype(bf16), "seq"), "seq", 0)

    block_part = dot(act_half, down_full, 1, 0).astype(bf16)
    block_out = hidden + scatter_sum(piece_of(block_part), "seq")
    down_part = dot(act_half, cot_all, 0, 0).astype(bf16)
    up_part = jnp.stack([dot(ffn_rows, d_gate, 0, 0), dot(ffn_rows, d_up, 0, 0)]).astype(bf16)

    d_mixed = dot(dmix_all, out_full, 1, 1)
    backs = [
        mixer_backward(dk, dv, *args, d_mixed[:, h * dv : (h + 1) * dv], saved[1:])
        for h, (args, saved) in enumerate(fronts)
    ]
    d_proj = jnp.concatenate([back[0] for back in backs], axis=1)
    d_gates = jnp.concatenate([back[1] for back in backs], axis=0).astype(bf16)
    taps_part = jnp.stack([back[2] for back in backs])
    d_small = jnp.stack([back[3] for back in backs])
    d_normed_part = (dot(d_proj, in_full, 1, 1) + dot(d_gates, gate_full, 0, 0)).astype(bf16)
    d_normed = scatter_sum(block_of(d_normed_part, "seq", 0), "seq")
    out_part = dot(mixed_half, dmix_all, 0, 0).astype(bf16)
    in_part = dot(rows_all, d_proj, 0, 0).astype(bf16)
    gate_part = dot(d_gates, rows_all, 1, 0)
    input_part, gain_one = norm_pull(d_normed)
    grad_input = d_hidden + input_part

    small_part = jnp.concatenate(
        [
            gate_part.reshape(heads * 2, fsdp, rows_d).transpose(1, 0, 2).reshape(fsdp, -1),
            taps_part.reshape(heads, KW, fsdp, taps_d).transpose(2, 0, 1, 3).reshape(fsdp, -1),
        ],
        axis=1,
    ).astype(bf16)
    in_grad = scatter_sum(block_of(in_part, "fsdp", 0), "fsdp").reshape(in_proj.shape)
    small_grad = scatter_sum(block_of(small_part, "fsdp", 0), "fsdp")
    gate_grad = small_grad[:, :gate_size].reshape(heads, 2, rows_d).transpose(2, 0, 1)
    conv_grad = small_grad[:, gate_size:].reshape(heads, KW, taps_d).transpose(1, 0, 2)
    out_grad = scatter_sum(block_of(out_part, "fsdp", 1), "fsdp").reshape(out_proj.shape)
    up_grad = scatter_sum(block_of(up_part, "fsdp", 1), "fsdp").transpose(1, 0, 2)
    down_grad = scatter_sum(block_of(down_part, "fsdp", 1), "fsdp")

    heads_total = decay_log.shape[0]
    spread = lax.dynamic_update_slice_in_dim(
        jnp.zeros((2, heads_total), f32), d_small[:, 1:, 0].T, head_start, 1
    )
    sums = jnp.concatenate(
        [gain_one, gain_two, jnp.sum(d_small[:, 0], axis=0), spread.reshape(-1)]
    )[None]
    sums = tree_sum(tree_sum(sums, "fsdp"), "seq")[0]
    gains_grad = sums[: 2 * model].reshape(2, model)
    head_grad = sums[2 * model : 2 * model + dv]
    decay_grad = sums[2 * model + dv : 2 * model + dv + heads_total]
    bias_grad = sums[2 * model + dv + heads_total :]

    params = (in_proj, gate_proj, conv_taps, out_proj, ffn_up, ffn_down, norm_gains, head_gain,
              decay_log, step_bias)
    means = (in_mean, gate_mean, conv_mean, out_mean, up_mean, down_mean, gains_mean, head_mean,
             decay_mean, bias_mean)
    squares = (in_square, gate_square, conv_square, out_square, up_square, down_square,
               gains_square, head_square, decay_square, bias_square)
    grads = (in_grad, gate_grad, conv_grad, out_grad, up_grad, down_grad, gains_grad, head_grad,
             decay_grad, bias_grad)
    results = [block_out[None], grad_input[None]]
    for param, mean, square, grad in zip(params, means, squares, grads):
        weight_next, mean_next, square_next = adam_step(param, mean, square, grad)
        results.extend([grad, weight_next, mean_next, square_next])
    return tuple(results)


def solution(mesh):
    tokens = P("fsdp", "seq", None)
    whole = P("fsdp", None)
    weights = (
        tokens, tokens, P(None, "seq", "fsdp"), P("seq", None, "fsdp"), P("fsdp", None, "seq"),
        P("seq", "fsdp"),
    ) + (P(),) * 4
    ins = (tokens, tokens, whole, whole) + tuple(s for s in weights for _ in range(3))
    outs = (tokens, tokens) + tuple(s for s in weights for _ in range(4))
    return jax.shard_map(per_device, mesh=mesh, in_specs=ins, out_specs=outs, check_vma=False)
```
